1024 devices in a mesh: pipe: 32 (over z), expert: 8 (over x_hi, y), dp: 4 (over x_lo, core).
Axes of the slice: x: 4 (x_hi: 2, x_lo: 2; x = x_hi * 2 + x_lo), y: 4, z: 32, core: 2. Of those that a mesh axis runs over, the one named last changes fastest.
Arguments:
- enter_fwd: bfloat16 [32, 1024, 7168], P('pipe', 'expert', 'dp'), may hold values from -6 to 6
- enter_rev: bfloat16 [32, 1024, 7168], P('pipe', 'expert', 'dp'), may hold values from -6 to 6
- cot_rev: bfloat16 [32, 1024, 7168], P('pipe', 'expert', 'dp'), may hold values from -0.1875 to 0.1875
- gain: bfloat16 [2, 32, 7168], P(None, 'pipe', 'dp'), may hold values from 0.5 to 1.5
- proj_down: bfloat16 [2, 32, 256, 7168], P(None, 'pipe', None, 'dp'), may hold values from -0.0625 to 0.0625
- proj_up: bfloat16 [2, 32, 256, 7168], P(None, 'pipe', None, 'dp'), may hold values from -0.375 to 0.375
- master: float32 [2, 32, 256, 7168], P(None, 'pipe', 'expert', 'dp'), may hold values from -0.125 to 0.125
- moment: bfloat16 [2, 32, 256, 7168], P(None, 'pipe', 'expert', 'dp'), may hold values from -6 to 6
- second: bfloat16 [2, 32, 256, 7168], P(None, 'pipe', 'expert', 'dp'), may hold values from 0.5 to 20
Outputs:
- leave_fwd: bfloat16 [32, 1024, 7168], P('pipe', 'expert', 'dp')
- codes: bfloat16 [2, 32, 256, 7168], P(None, 'pipe', 'expert', 'dp')
- scales: float32 [2, 32, 2, 56], P(None, 'pipe', None, 'dp')
The draws below stay inside these ranges and needn't reach their ends.
All inputs are finite; a program needn't handle non-finite values.
Results may differ from the reference program's by a relative error of at most 0.0047.
The reference program's roundings to bfloat16 on the way count: a program that leaves them out, or rounds other values in their place, can miss the bound.
Values may be sent and summed in bfloat16 or wider, within the bound.
A program may use at most 32 MiB of HBM per device.

```python
import math
import jax
import jax.numpy as jnp
from jax import lax

D = 7168
LATENT = 256
TOK_DEV = 128
SECTIONS = 32
TOKENS = 1024
N_EXPERT = 8


def block_levels(own_key, extent, split, smallest, top_value):
    loudness, own = 1.0, jax.random.fold_in(own_key, 6)
    for position, shards_of in split:
        heights = jnp.exp(jax.random.uniform(jax.random.fold_in(own, position), (shards_of,), jnp.float32, smallest / len(split), top_value / len(split)))
        loudness = loudness * jnp.repeat(heights, extent[position] // shards_of).reshape([-1 if axis == position else 1 for axis in range(len(extent))])
    return loudness


def scatter_about(rng, extent, scale, limit, split=(), held_as=jnp.bfloat16):
    loudness = block_levels(rng, extent, split, -0.22, 0.18) if split else 1.0
    drawn = jax.random.normal(rng, extent, jnp.float32) * scale * loudness
    return jnp.minimum(jnp.maximum(drawn, -limit), limit).astype(held_as)


def setup_inputs(seed: int = 0) -> dict:
    key_list = jax.random.split(jax.random.key(seed), 10)
    return {
        "enter_fwd": scatter_about(key_list[0], (SECTIONS, TOKENS, D), 1.0, 6.0, ((0, 32), (1, 8), (2, 4))),
        "enter_rev": scatter_about(key_list[1], (SECTIONS, TOKENS, D), 1.0, 6.0, ((0, 32), (1, 8), (2, 4))),
        "cot_rev": scatter_about(key_list[2], (SECTIONS, TOKENS, D), 0.03, 0.1875, ((0, 32), (1, 8), (2, 4))),
        "gain": jnp.clip(1.0 + 0.1 * jax.random.normal(key_list[3], (2, SECTIONS, D), jnp.float32), 0.5, 1.5).astype(jnp.bfloat16),
        "proj_down": scatter_about(key_list[4], (2, SECTIONS, LATENT, D), D ** -0.5, 0.0625, ((1, 32), (3, 4))),
        "proj_up": scatter_about(key_list[5], (2, SECTIONS, LATENT, D), LATENT ** -0.5, 0.375, ((1, 32), (3, 4))),
        "master": scatter_about(key_list[6], (2, SECTIONS, LATENT, D), 0.02, 0.125, ((1, 32), (2, 8), (3, 4)), jnp.float32),
        "moment": scatter_about(key_list[7], (2, SECTIONS, LATENT, D), 1.0, 6.0, ((1, 32), (2, 8), (3, 4))),
        "second": jnp.clip(jnp.exp(math.log(20.0) - 3.6888795 * jax.random.uniform(key_list[8], (2, SECTIONS, LATENT, D), jnp.float32) ** block_levels(key_list[8], (2, SECTIONS, LATENT, D), ((1, 32), (2, 8), (3, 4)), -0.2, 0.2)), 0.5, 20.0).astype(jnp.bfloat16),
    }


def prepare(rows, gain_row, down):
    scaled = (rows.astype(jnp.float32) * gain_row).astype(jnp.bfloat16)
    squares = lax.optimization_barrier(jnp.sum(jnp.square(rows.astype(jnp.float32)), axis=-1))
    raw = jnp.dot(scaled, down.T, preferred_element_type=jnp.float32)
    rscale = lax.rsqrt(squares / D + 1e-06)
    return (scaled, raw, rscale)

def pick(array, first, index):
    return lax.dynamic_index_in_dim(array[first], index, 0, keepdims=False)

def reference(enter_fwd, enter_rev, cot_rev, gain, proj_down, proj_up, master, moment, second):

    def section(index):
        mirror_index = (SECTIONS - 1 - index).astype(jnp.int32)
        fwd_rows = lax.dynamic_index_in_dim(enter_fwd, index, 0, keepdims=False)
        back_rows = lax.dynamic_index_in_dim(enter_rev, mirror_index, 0, keepdims=False)
        back_cot = lax.dynamic_index_in_dim(cot_rev, mirror_index, 0, keepdims=False)
        own_gain = pick(gain, 0, index).astype(jnp.float32)
        own_down = pick(proj_down, 0, index)
        own_upper = pick(proj_up, 0, index)
        copy_gain = pick(gain, 1, mirror_index).astype(jnp.float32)
        copy_down = pick(proj_down, 1, mirror_index)
        copy_upper = pick(proj_up, 1, mirror_index)
        fwd_scaled, fwd_raw, fwd_r = prepare(fwd_rows, own_gain, own_down)
        hidden_one = (fwd_raw * fwd_r[:, None]).astype(jnp.bfloat16)
        result = (fwd_rows.astype(jnp.float32) + jnp.dot(hidden_one, own_upper, preferred_element_type=jnp.float32)).astype(jnp.bfloat16)
        back_scaled, back_raw, back_r = prepare(back_rows, copy_gain, copy_down)
        hidden_two = (back_raw * back_r[:, None]).astype(jnp.bfloat16)
        back_dlat = jnp.dot(back_cot, copy_upper.T, preferred_element_type=jnp.float32)
        error = (back_dlat * back_r[:, None]).astype(jnp.bfloat16)
        error_groups = error.astype(jnp.float32).reshape(N_EXPERT, TOK_DEV, LATENT)
        hidden_groups = hidden_two.astype(jnp.float32).reshape(N_EXPERT, TOK_DEV, LATENT)
        scaled_groups = back_scaled.astype(jnp.float32).reshape(N_EXPERT, TOK_DEV, D)
        cot_groups = back_cot.astype(jnp.float32).reshape(N_EXPERT, TOK_DEV, D)
        part_down = jnp.einsum('ktr,ktd->krd', error_groups, scaled_groups).astype(jnp.bfloat16)
        part_up = jnp.einsum('ktr,ktd->krd', hidden_groups, cot_groups).astype(jnp.bfloat16)
        part_down = lax.optimization_barrier(part_down)
        part_up = lax.optimization_barrier(part_up)
        partial_value = jnp.stack([lax.optimization_barrier(jnp.sum(part_down.astype(jnp.float32), axis=0)), lax.optimization_barrier(jnp.sum(part_up.astype(jnp.float32), axis=0))])
        share = lax.optimization_barrier(partial_value.astype(jnp.bfloat16))
        grad = share.astype(jnp.float32)
        weights = lax.dynamic_index_in_dim(master, index, 1, keepdims=False)
        first = lax.dynamic_index_in_dim(moment, index, 1, keepdims=False).astype(jnp.float32)
        secnd = lax.dynamic_index_in_dim(second, index, 1, keepdims=False).astype(jnp.float32)
        first = 0.9 * first + 0.1 * grad
        secnd = 0.95 * secnd + 0.05 * grad * grad
        update = first / (1.0 - 0.9 ** 10) / (jnp.sqrt(secnd / (1.0 - 0.95 ** 10)) + 1e-08)
        fresh = weights - 0.01 * (update + 0.1 * weights)
        blocks = jnp.abs(fresh).reshape(2, LATENT // 128, 128, D // 128, 128)
        block_scale = lax.optimization_barrier(jnp.max(blocks, axis=(2, 4))) + 1e-06
        expanded = jnp.repeat(jnp.repeat(block_scale, 128, axis=1), 128, axis=2)
        coded = (fresh / expanded).astype(jnp.bfloat16)
        return (result, coded, block_scale)
    results, coded, block_scale = lax.map(section, jnp.arange(SECTIONS, dtype=jnp.int32))
    leave_fwd = jnp.concatenate([jnp.zeros((1, TOKENS, D), jnp.bfloat16), results[:-1]], axis=0)
    return (leave_fwd, jnp.moveaxis(coded, 0, 1), jnp.moveaxis(block_scale, 0, 1))
```

```python
import functools

import jax
import jax.numpy as jnp
from jax import lax
from jax.experimental import pallas as pl
from jax.experimental.pallas import tpu as pltpu
from jax.sharding import PartitionSpec as P

D = 7168
CW = 256
F32 = jnp.float32
BF16 = jnp.bfloat16
MESH = pl.DeviceIdType.MESH
NT = (((1,), (1,)), ((), ()))


def kernel(
    sections, chunks,
    x1_hbm, x2_hbm, c2_hbm, gain_hbm, down_hbm, up_hbm, master_hbm, moment_hbm, second_hbm,
    leave_hbm, codes_hbm, scales_ref,
    x1, x2, c2, gain, down, up, master, moment, second,
    xg2, part, core_got, chip_sum, near_got, lat, sq, sq_got, rows_r,
    ybuf, turned, grads, group_got, share, mirror_got, fresh, peak, peak_got, coded,
    load_sem, core_send, core_recv, near_send, near_recv, lat_send, lat_recv, sq_send, sq_recv,
    y_send, y_recv, zero_sem, group_send, group_recv, mirror_send, mirror_recv,
    peak_send, peak_recv, code_sem,
):
    pipe = lax.axis_index("pipe")
    expert = lax.axis_index("expert")
    dp = lax.axis_index("dp")
    core = lax.rem(dp, 2)
    other_core = {"dp": dp + 1 - 2 * core}
    near = {"dp": lax.rem(dp + 2, 4)}
    near_other = {"dp": 3 - dp}
    x_hi = expert // 4
    y = lax.rem(expert, 4)
    mirror = {"pipe": sections - 1 - pipe}
    following = {"pipe": lax.rem(pipe + 1, sections)}
    previous = {"pipe": lax.rem(pipe + sections - 1, sections)}
    peers = []
    for dx in range(2):
        for dy in range(4):
            if dx or dy:
                peers.append(lax.rem(x_hi + dx, 2) * 4 + lax.rem(y + dy, 4))

    loads = [
        (x1_hbm, x1), (gain_hbm, gain), (down_hbm.at[0], down.at[0]),
        (x2_hbm, x2), (down_hbm.at[1], down.at[1]), (c2_hbm, c2), (up_hbm.at[1], up.at[1]),
        (up_hbm.at[0], up.at[0]), (master_hbm, master), (moment_hbm, moment), (second_hbm, second),
    ]
    copies = [pltpu.make_async_copy(s, d, load_sem.at[i]) for i, (s, d) in enumerate(loads)]
    for copy in copies:
        copy.start()

    barrier = pltpu.get_barrier_semaphore()
    others = [other_core, near, near_other, mirror, following, previous]
    others += [{"expert": peer} for peer in peers]
    for device in others:
        pl.semaphore_signal(barrier, inc=1, device_id=device, device_id_type=MESH)

    def send(src, dst, send_sem, recv_sem, device):
        copy = pltpu.make_async_remote_copy(
            src_ref=src, dst_ref=dst, send_sem=send_sem, recv_sem=recv_sem,
            device_id=device, device_id_type=MESH,
        )
        copy.start()
        return copy

    def spread(column):
        return jnp.broadcast_to(column, (128, 128)).T[0:8]

    def project(rows_ref, gain_row, weights):
        rows = rows_ref[...].astype(F32)
        scaled = (rows * gain_row).astype(BF16)
        raw = lax.dot_general(scaled, weights, NT, preferred_element_type=F32)
        return scaled, raw, jnp.sum(rows * rows, axis=1, keepdims=True)

    for i in range(3):
        copies[i].wait()
    _, raw, square = project(x1, gain[0:1, :].astype(F32), down[0])
    part[0] = raw.reshape(2, 64, 256)
    sq[0] = spread(square)
    for i in range(3, 5):
        copies[i].wait()
    scaled, raw, square = project(x2, gain[1:2, :].astype(F32), down[1])
    xg2[...] = scaled
    part[1] = raw.reshape(2, 64, 256)
    sq[1] = spread(square)
    for i in range(5, 7):
        copies[i].wait()
    raw = lax.dot_general(c2[...], up[1], NT, preferred_element_type=F32)
    part[2] = raw.reshape(2, 64, 256)

    pl.semaphore_wait(barrier, len(others))

    pending = []
    for i in range(3):
        pending.append(send(part.at[i, 1 - core], core_got.at[i], core_send.at[i], core_recv.at[i], other_core))
    for i, device in enumerate((other_core, near, near_other)):
        pending.append(send(sq, sq_got.at[i], sq_send.at[i], sq_recv.at[i], device))
    near_copies = []
    for i in range(3):
        pending[i].wait_recv()
        chip_sum[i] = part[i, core] + core_got[i]
        near_copies.append(send(chip_sum.at[i], near_got.at[i], near_send.at[i], near_recv.at[i], near))
    for i in range(3, 6):
        pending[i].wait_recv()
    for s in range(2):
        total = (sq[s] + sq_got[0, s]) + (sq_got[1, s] + sq_got[2, s])
        scale = lax.rsqrt(total / D + 1e-06)
        turned_rows = jnp.broadcast_to(scale[0:1], (128, 128)).T
        rows_r[s] = turned_rows.reshape(2, 64, 128)
    lat_copies = []
    for i in range(3):
        near_copies[i].wait_recv()
        r = rows_r[min(i, 1), core]
        total = chip_sum[i] + near_got[i]
        lat[i, core] = (total * jnp.concatenate([r, r], axis=1)).astype(BF16)
        lat_copies.append(send(lat.at[i, core], lat.at[i, core], lat_send.at[i], lat_recv.at[i], other_core))

    copies[7].wait()
    lat_copies[0].wait_recv()
    hidden = lat[0].reshape(128, 256)

    def columns(k):
        return pl.ds(pl.multiple_of(k * CW, CW), CW)

    def y_copy(k):
        return pltpu.make_async_remote_copy(
            src_ref=ybuf.at[k], dst_ref=leave_hbm.at[:, columns(k)],
            send_sem=y_send.at[k], recv_sem=y_recv.at[k],
            device_id=following, device_id_type=MESH,
        )

    @pl.loop(0, chunks)
    def _(k):
        wide = jnp.dot(hidden, up[0, :, columns(k)], preferred_element_type=F32)
        ybuf[k] = (x1[:, columns(k)].astype(F32) + wide).astype(BF16)

        @pl.when(pipe < sections - 1)
        def _():
            y_copy(k).start()

    for i in (1, 2):
        lat_copies[i].wait_recv()
        turned[i - 1] = lat[i].reshape(128, 256).astype(F32).T.astype(BF16)

    @pl.loop(0, chunks)
    def _(k):
        grad_down = jnp.dot(turned[1], xg2[:, columns(k)], preferred_element_type=F32)
        grads[k, :, 0:32, :] = grad_down.astype(BF16).reshape(8, 32, CW)
        grad_up = jnp.dot(turned[0], c2[:, columns(k)], preferred_element_type=F32)
        grads[k, :, 32:64, :] = grad_up.astype(BF16).reshape(8, 32, CW)
        for slot, peer in enumerate(peers):
            send(grads.at[k, peer], group_got.at[k, slot], group_send.at[k], group_recv.at[k], {"expert": peer})

    def mirror_copy(k):
        return pltpu.make_async_remote_copy(
            src_ref=share.at[k], dst_ref=mirror_got.at[k],
            send_sem=mirror_send.at[k], recv_sem=mirror_recv.at[k],
            device_id=mirror, device_id_type=MESH,
        )

    @pl.loop(0, chunks)
    def _(k):
        pltpu.make_async_copy(group_got.at[k], group_got.at[k], group_recv.at[k]).wait()
        total = grads[k, expert].astype(F32)
        for slot in range(7):
            total = total + group_got[k, slot].astype(F32)
        share[k] = total.astype(BF16)
        mirror_copy(k).start()

    for i in range(8, 11):
        copies[i].wait()

    def update(k):
        mirror_copy(k).wait_recv()
        grad = mirror_got[k].astype(F32)
        first = 0.9 * moment[:, columns(k)].astype(F32) + 0.1 * grad
        secnd = 0.95 * second[:, columns(k)].astype(F32) + 0.05 * grad * grad
        step = first / (1.0 - 0.9**10) / (jnp.sqrt(secnd / (1.0 - 0.95**10)) + 1e-08)
        old = master[:, columns(k)]
        new = old - 0.01 * (step + 0.1 * old)
        fresh[k] = new
        size = jnp.abs(new)
        top = jnp.broadcast_to(jnp.max(size[0:32], axis=0, keepdims=True), (8, CW))
        low = jnp.broadcast_to(jnp.max(size[32:64], axis=0, keepdims=True), (8, CW))
        row = lax.broadcasted_iota(jnp.int32, (8, CW), 0)
        peak[k] = jnp.where(row < 4, top, low)
        for slot, peer in enumerate(peers):
            send(peak.at[k], peak_got.at[k, slot], peak_send.at[k], peak_recv.at[k], {"expert": peer})

    lane = lax.broadcasted_iota(jnp.int32, (8, 128), 1)

    def code_copy(k):
        return pltpu.make_async_copy(coded.at[k], codes_hbm.at[:, columns(k)], code_sem.at[k])

    def finish(k, tables):
        pltpu.make_async_copy(peak_got.at[k], peak_got.at[k], peak_recv.at[k]).wait()
        mine = peak[k]
        for slot in range(3):
            mine = jnp.maximum(mine, peak_got[k, slot])
        theirs = peak_got[k, 3]
        for slot in range(4, 7):
            theirs = jnp.maximum(theirs, peak_got[k, slot])
        mine_table, their_table = tables
        for block in range(CW // 128):
            cols = slice(block * 128, block * 128 + 128)
            own = jnp.max(mine[:, cols], axis=1, keepdims=True) + 1e-06
            far = jnp.max(theirs[:, cols], axis=1, keepdims=True) + 1e-06
            here = lane == k * (CW // 128) + block
            mine_table = jnp.where(here, own, mine_table)
            their_table = jnp.where(here, far, their_table)
            coded[k, 0:32, cols] = (fresh[k, 0:32, cols] / own[0:1]).astype(BF16)
            coded[k, 32:64, cols] = (fresh[k, 32:64, cols] / own[4:5]).astype(BF16)
        code_copy(k).start()
        return mine_table, their_table

    update(0)
    empty = jnp.zeros((8, 128), F32)

    def both(k, tables):
        update(k)
        return finish(k - 1, tables)

    tables = lax.fori_loop(1, chunks, both, (empty, empty))
    mine_table, their_table = finish(chunks - 1, tables)
    width = scales_ref.shape[-1]
    for m in range(2):
        for rb in range(2):
            row = jnp.where(x_hi == rb, mine_table[4 * m : 4 * m + 1], their_table[4 * m : 4 * m + 1])
            scales_ref[m, rb : rb + 1, :] = row[:, 0:width]

    for copy in pending + near_copies + lat_copies:
        copy.wait_send()

    @pl.when(pipe == 0)
    def _():
        ybuf_zero = jnp.zeros((128, CW), BF16)

        @pl.loop(0, chunks)
        def _(k):
            y_copy(k).wait_send()
            ybuf[k] = ybuf_zero
            copy = pltpu.make_async_copy(ybuf.at[k], leave_hbm.at[:, columns(k)], zero_sem)
            copy.start()
            copy.wait()

    @pl.when(pipe > 0)
    def _():
        @pl.loop(0, chunks)
        def _(k):
            y_copy(k).wait_recv()

            @pl.when(pipe < sections - 1)
            def _():
                y_copy(k).wait_send()

    @pl.loop(0, chunks)
    def _(k):
        pltpu.make_async_copy(group_got.at[k], group_got.at[k], group_send.at[k]).wait()
        pltpu.make_async_copy(peak_got.at[k], peak_got.at[k], peak_send.at[k]).wait()
        mirror_copy(k).wait_send()
        code_copy(k).wait()


def solution(mesh):
    sections = mesh.shape["pipe"]

    def shards(enter_fwd, enter_rev, cot_rev, gain, proj_down, proj_up, master, moment, second):
        width = enter_fwd.shape[-1]
        tokens = enter_fwd.shape[1]
        latent = proj_down.shape[2]
        rows = master.shape[2]
        chunks = width // CW
        any_spec = pl.BlockSpec(memory_space=pl.ANY)
        dma = pltpu.SemaphoreType.DMA
        leave, codes, scales = pl.pallas_call(
            functools.partial(kernel, sections, chunks),
            out_shape=(
                jax.ShapeDtypeStruct((tokens, width), BF16),
                jax.ShapeDtypeStruct((2 * rows, width), BF16),
                jax.ShapeDtypeStruct((2, 2, width // 128), F32),
            ),
            in_specs=[any_spec] * 9,
            out_specs=(any_spec, any_spec, pl.BlockSpec(memory_space=pltpu.VMEM)),
            scratch_shapes=[
                pltpu.VMEM((tokens, width), BF16),
                pltpu.VMEM((tokens, width), BF16),
                pltpu.VMEM((tokens, width), BF16),
                pltpu.VMEM((2, width), BF16),
                pltpu.VMEM((2, latent, width), BF16),
                pltpu.VMEM((2, latent, width), BF16),
                pltpu.VMEM((2 * rows, width), F32),
                pltpu.VMEM((2 * rows, width), BF16),
                pltpu.VMEM((2 * rows, width), BF16),
                pltpu.VMEM((tokens, width), BF16),
                pltpu.VMEM((3, 2, 64, 256), F32),
                pltpu.VMEM((3, 64, 256), F32),
                pltpu.VMEM((3, 64, 256), F32),
                pltpu.VMEM((3, 64, 256), F32),
                pltpu.VMEM((3, 2, 64, 256), BF16),
                pltpu.VMEM((2, 8, 128), F32),
                pltpu.VMEM((3, 2, 8, 128), F32),
                pltpu.VMEM((2, 2, 64, 128), F32),
                pltpu.VMEM((chunks, tokens, CW), BF16),
                pltpu.VMEM((2, 256, 128), BF16),
                pltpu.VMEM((chunks, 8, 64, CW), BF16),
                pltpu.VMEM((chunks, 7, 64, CW), BF16),
                pltpu.VMEM((chunks, 64, CW), BF16),
                pltpu.VMEM((chunks, 64, CW), BF16),
                pltpu.VMEM((chunks, 64, CW), F32),
                pltpu.VMEM((chunks, 8, CW), F32),
                pltpu.VMEM((chunks, 7, 8, CW), F32),
                pltpu.VMEM((chunks, 64, CW), BF16),
                dma((11,)),
                dma((3,)), dma((3,)), dma((3,)), dma((3,)), dma((3,)), dma((3,)), dma((3,)), dma((3,)),
                dma((chunks,)), dma((chunks,)), dma,
                dma((chunks,)), dma((chunks,)), dma((chunks,)), dma((chunks,)),
                dma((chunks,)), dma((chunks,)), dma((chunks,)),
            ],
            compiler_params=pltpu.CompilerParams(collective_id=0, has_side_effects=True),
            name="section_pair",
        )(
            enter_fwd.reshape(tokens, width),
            enter_rev.reshape(tokens, width),
            cot_rev.reshape(tokens, width),
            gain.reshape(2, width),
            proj_down.reshape(2, latent, width),
            proj_up.reshape(2, latent, width),
            master.reshape(2 * rows, width),
            moment.reshape(2 * rows, width),
            second.reshape(2 * rows, width),
        )
        return (
            leave.reshape(1, tokens, width),
            codes.reshape(2, 1, rows, width),
            scales.reshape(2, 1, 2, width // 128),
        )

    in_specs = (
        P("pipe", "expert", "dp"),
        P("pipe", "expert", "dp"),
        P("pipe", "expert", "dp"),
        P(None, "pipe", "dp"),
        P(None, "pipe", None, "dp"),
        P(None, "pipe", None, "dp"),
        P(None, "pipe", "expert", "dp"),
        P(None, "pipe", "expert", "dp"),
        P(None, "pipe", "expert", "dp"),
    )
    out_specs = (
        P("pipe", "expert", "dp"),
        P(None, "pipe", "expert", "dp"),
        P(None, "pipe", None, "dp"),
    )
    return jax.shard_map(shards, mesh=mesh, in_specs=in_specs, out_specs=out_specs, check_vma=False)
```

```python
import functools

import jax
import jax.numpy as jnp
from jax import lax
from jax.experimental import pallas as pl
from jax.experimental.pallas import tpu as pltpu
from jax.sharding import PartitionSpec as P

D = 7168
CW = 256
F32 = jnp.float32
BF16 = jnp.bfloat16
MESH = pl.DeviceIdType.MESH
NT = (((1,), (1,)), ((), ()))


def kernel(
    sections, chunks,
    x1_hbm, x2_hbm, c2_hbm, gain_hbm, down_hbm, up_hbm, master_hbm, moment_hbm, second_hbm,
    leave, coded, scales_ref,
    x1, x2, c2, gain, down, up, master, moment, second,
    xg2, part, core_got, chip_sum, near_got, lat, sq, sq_got, rows_r,
    ybuf, turned, grads, group_got, share, mirror_got, fresh, peak, peak_got,
    load_sem, core_send, core_recv, near_send, near_recv, lat_send, lat_recv, sq_send, sq_recv,
    y_send, y_recv, group_send, group_recv, mirror_send, mirror_recv,
    peak_send, peak_recv,
):
    pipe = lax.axis_index("pipe")
    expert = lax.axis_index("expert")
    dp = lax.axis_index("dp")
    core = lax.rem(dp, 2)
    other_core = {"dp": dp + 1 - 2 * core}
    near = {"dp": lax.rem(dp + 2, 4)}
    near_other = {"dp": 3 - dp}
    x_hi = expert // 4
    y = lax.rem(expert, 4)
    mirror = {"pipe": sections - 1 - pipe}
    following = {"pipe": lax.rem(pipe + 1, sections)}
    previous = {"pipe": lax.rem(pipe + sections - 1, sections)}
    peers = []
    for dx in range(2):
        for dy in range(4):
            if dx or dy:
                peers.append(lax.rem(x_hi + dx, 2) * 4 + lax.rem(y + dy, 4))

    loads = [
        (x2_hbm, x2), (gain_hbm, gain), (down_hbm.at[1], down.at[1]), (c2_hbm, c2), (up_hbm.at[1], up.at[1]),
        (x1_hbm, x1), (down_hbm.at[0], down.at[0]), (up_hbm.at[0], up.at[0]),
        (master_hbm, master), (moment_hbm, moment), (second_hbm, second),
    ]
    copies = [pltpu.make_async_copy(s, d, load_sem.at[i]) for i, (s, d) in enumerate(loads)]
    for copy in copies:
        copy.start()

    barrier = pltpu.get_barrier_semaphore()
    others = [other_core, near, near_other, mirror, following, previous]
    others += [{"expert": peer} for peer in peers]
    for device in others:
        pl.semaphore_signal(barrier, inc=1, device_id=device, device_id_type=MESH)

    def send(src, dst, send_sem, recv_sem, device):
        copy = pltpu.make_async_remote_copy(
            src_ref=src, dst_ref=dst, send_sem=send_sem, recv_sem=recv_sem,
            device_id=device, device_id_type=MESH,
        )
        copy.start()
        return copy

    def spread(column):
        return jnp.broadcast_to(column, (128, 128)).T[0:8]

    def project(rows_ref, gain_row, weights):
        rows = rows_ref[...].astype(F32)
        scaled = (rows * gain_row).astype(BF16)
        raw = lax.dot_general(scaled, weights, NT, preferred_element_type=F32)
        return scaled, raw, jnp.sum(rows * rows, axis=1, keepdims=True)

    for i in range(3):
        copies[i].wait()
    scaled, raw, square = project(x2, gain[1:2, :].astype(F32), down[1])
    xg2[...] = scaled
    part[1] = raw.reshape(2, 64, 256)
    sq[1] = spread(square)
    for i in range(3, 5):
        copies[i].wait()
    raw = lax.dot_general(c2[...], up[1], NT, preferred_element_type=F32)
    part[2] = raw.reshape(2, 64, 256)

    pl.semaphore_wait(barrier, len(others))

    core_copies, near_copies, lat_copies, sq_copies = {}, {}, {}, {}

    def to_core(i):
        core_copies[i] = send(part.at[i, 1 - core], core_got.at[i], core_send.at[i], core_recv.at[i], other_core)

    def squares(s):
        for i, device in enumerate((other_core, near, near_other)):
            sq_copies[s, i] = send(sq.at[s], sq_got.at[i, s], sq_send.at[s, i], sq_recv.at[s, i], device)

    def to_near(i):
        core_copies[i].wait_recv()
        chip_sum[i] = part[i, core] + core_got[i]
        near_copies[i] = send(chip_sum.at[i], near_got.at[i], near_send.at[i], near_recv.at[i], near)

    def norms(s):
        for i in range(3):
            sq_copies[s, i].wait_recv()
        total = (sq[s] + sq_got[0, s]) + (sq_got[1, s] + sq_got[2, s])
        scale = lax.rsqrt(total / D + 1e-06)
        rows_r[s] = jnp.broadcast_to(scale[0:1], (128, 128)).T.reshape(2, 64, 128)

    def latents(i):
        near_copies[i].wait_recv()
        r = rows_r[min(i, 1), core]
        total = chip_sum[i] + near_got[i]
        lat[i, core] = (total * jnp.concatenate([r, r], axis=1)).astype(BF16)
        lat_copies[i] = send(lat.at[i, core], lat.at[i, core], lat_send.at[i], lat_recv.at[i], other_core)

    to_core(1)
    to_core(2)
    squares(1)
    for i in range(5, 7):
        copies[i].wait()
    _, raw, square = project(x1, gain[0:1, :].astype(F32), down[0])
    part[0] = raw.reshape(2, 64, 256)
    sq[0] = spread(square)
    to_core(0)
    squares(0)
    to_near(1)
    to_near(2)
    to_near(0)
    norms(1)
    latents(1)
    latents(2)

    def columns(k):
        return pl.ds(pl.multiple_of(k * CW, CW), CW)

    for i in (1, 2):
        lat_copies[i].wait_recv()
        turned[i - 1] = lat[i].reshape(128, 256).astype(F32).T.astype(BF16)

    @pl.loop(0, chunks)
    def _(k):
        grad_down = jnp.dot(turned[1], xg2[:, columns(k)], preferred_element_type=F32)
        grads[k, :, 0:32, :] = grad_down.astype(BF16).reshape(8, 32, CW)
        grad_up = jnp.dot(turned[0], c2[:, columns(k)], preferred_element_type=F32)
        grads[k, :, 32:64, :] = grad_up.astype(BF16).reshape(8, 32, CW)
        for slot, peer in enumerate(peers):
            send(grads.at[k, peer], group_got.at[k, slot], group_send.at[k], group_recv.at[k], {"expert": peer})

    copies[7].wait()
    norms(0)
    latents(0)
    lat_copies[0].wait_recv()
    hidden = lat[0].reshape(128, 256)

    def y_copy(k):
        return pltpu.make_async_remote_copy(
            src_ref=ybuf.at[k], dst_ref=leave.at[k],
            send_sem=y_send.at[k], recv_sem=y_recv.at[k],
            device_id=following, device_id_type=MESH,
        )

    @pl.loop(0, chunks)
    def _(k):
        wide = jnp.dot(hidden, up[0, :, columns(k)], preferred_element_type=F32)
        ybuf[k] = (x1[:, columns(k)].astype(F32) + wide).astype(BF16)

        @pl.when(pipe < sections - 1)
        def _():
            y_copy(k).start()

    def mirror_copy(k):
        return pltpu.make_async_remote_copy(
            src_ref=share.at[k], dst_ref=mirror_got.at[k],
            send_sem=mirror_send.at[k], recv_sem=mirror_recv.at[k],
            device_id=mirror, device_id_type=MESH,
        )

    @pl.loop(0, chunks)
    def _(k):
        pltpu.make_async_copy(group_got.at[k], group_got.at[k], group_recv.at[k]).wait()
        total = grads[k, expert].astype(F32)
        for slot in range(7):
            total = total + group_got[k, slot].astype(F32)
        share[k] = total.astype(BF16)
        mirror_copy(k).start()

    for i in range(8, 11):
        copies[i].wait()

    def update(k):
        mirror_copy(k).wait_recv()
        grad = mirror_got[k].astype(F32)
        first = 0.9 * moment[:, columns(k)].astype(F32) + 0.1 * grad
        secnd = 0.95 * second[:, columns(k)].astype(F32) + 0.05 * grad * grad
        step = first / (1.0 - 0.9**10) / (jnp.sqrt(secnd / (1.0 - 0.95**10)) + 1e-08)
        old = master[:, columns(k)]
        new = old - 0.01 * (step + 0.1 * old)
        fresh[k] = new
        size = jnp.abs(new)
        top = jnp.broadcast_to(jnp.max(size[0:32], axis=0, keepdims=True), (8, CW))
        low = jnp.broadcast_to(jnp.max(size[32:64], axis=0, keepdims=True), (8, CW))
        row = lax.broadcasted_iota(jnp.int32, (8, CW), 0)
        peak[k] = jnp.where(row < 4, top, low)
        for slot, peer in enumerate(peers):
            send(peak.at[k], peak_got.at[k, slot], peak_send.at[k], peak_recv.at[k], {"expert": peer})

    lane = lax.broadcasted_iota(jnp.int32, (8, 128), 1)

    def finish(k, tables):
        pltpu.make_async_copy(peak_got.at[k], peak_got.at[k], peak_recv.at[k]).wait()
        mine = peak[k]
        for slot in range(3):
            mine = jnp.maximum(mine, peak_got[k, slot])
        theirs = peak_got[k, 3]
        for slot in range(4, 7):
            theirs = jnp.maximum(theirs, peak_got[k, slot])
        mine_table, their_table = tables
        for block in range(CW // 128):
            cols = slice(block * 128, block * 128 + 128)
            own = jnp.max(mine[:, cols], axis=1, keepdims=True) + 1e-06
            far = jnp.max(theirs[:, cols], axis=1, keepdims=True) + 1e-06
            here = lane == k * (CW // 128) + block
            mine_table = jnp.where(here, own, mine_table)
            their_table = jnp.where(here, far, their_table)
            coded[k, 0:32, cols] = (fresh[k, 0:32, cols] / own[0:1]).astype(BF16)
            coded[k, 32:64, cols] = (fresh[k, 32:64, cols] / own[4:5]).astype(BF16)
        return mine_table, their_table

    @pl.loop(0, chunks)
    def _(k):
        update(k)

    empty = jnp.zeros((8, 128), F32)
    mine_table, their_table = lax.fori_loop(0, chunks, finish, (empty, empty))
    width = scales_ref.shape[-1]
    for m in range(2):
        for rb in range(2):
            row = jnp.where(x_hi == rb, mine_table[4 * m : 4 * m + 1], their_table[4 * m : 4 * m + 1])
            scales_ref[m, rb : rb + 1, :] = row[:, 0:width]

    for group in (core_copies, near_copies, lat_copies, sq_copies):
        for copy in group.values():
            copy.wait_send()

    @pl.when(pipe == 0)
    def _():
        leave[...] = jnp.zeros_like(leave)

        @pl.loop(0, chunks)
        def _(k):
            y_copy(k).wait_send()

    @pl.when(pipe > 0)
    def _():
        @pl.loop(0, chunks)
        def _(k):
            y_copy(k).wait_recv()

            @pl.when(pipe < sections - 1)
            def _():
                y_copy(k).wait_send()

    @pl.loop(0, chunks)
    def _(k):
        pltpu.make_async_copy(group_got.at[k], group_got.at[k], group_send.at[k]).wait()
        pltpu.make_async_copy(peak_got.at[k], peak_got.at[k], peak_send.at[k]).wait()
        mirror_copy(k).wait_send()


def store(chunks, leave, coded, scales, leave_hbm, codes_hbm, scales_hbm, sem):
    copies = [pltpu.make_async_copy(scales, scales_hbm, sem.at[2 * chunks])]
    for k in range(chunks):
        cols = slice(k * CW, k * CW + CW)
        copies.append(pltpu.make_async_copy(leave.at[k], leave_hbm.at[:, cols], sem.at[2 * k]))
        copies.append(pltpu.make_async_copy(coded.at[k], codes_hbm.at[:, cols], sem.at[2 * k + 1]))
    for copy in copies:
        copy.start()
    for copy in copies:
        copy.wait()


def solution(mesh):
    sections = mesh.shape["pipe"]

    def shards(enter_fwd, enter_rev, cot_rev, gain, proj_down, proj_up, master, moment, second):
        width = enter_fwd.shape[-1]
        tokens = enter_fwd.shape[1]
        latent = proj_down.shape[2]
        rows = master.shape[2]
        chunks = width // CW
        any_spec = pl.BlockSpec(memory_space=pl.ANY)
        vmem_spec = pl.BlockSpec(memory_space=pltpu.VMEM)
        dma = pltpu.SemaphoreType.DMA
        leave, codes, scales = pl.pallas_call(
            functools.partial(kernel, sections, chunks),
            out_shape=(
                pltpu.VMEM((chunks, tokens, CW), BF16),
                pltpu.VMEM((chunks, 2 * rows, CW), BF16),
                pltpu.VMEM((2, 2, width // 128), F32),
            ),
            in_specs=[any_spec] * 9,
            out_specs=(vmem_spec,) * 3,
            scratch_shapes=[
                pltpu.VMEM((tokens, width), BF16),
                pltpu.VMEM((tokens, width), BF16),
                pltpu.VMEM((tokens, width), BF16),
                pltpu.VMEM((2, width), BF16),
                pltpu.VMEM((2, latent, width), BF16),
                pltpu.VMEM((2, latent, width), BF16),
                pltpu.VMEM((2 * rows, width), F32),
                pltpu.VMEM((2 * rows, width), BF16),
                pltpu.VMEM((2 * rows, width), BF16),
                pltpu.VMEM((tokens, width), BF16),
                pltpu.VMEM((3, 2, 64, 256), F32),
                pltpu.VMEM((3, 64, 256), F32),
                pltpu.VMEM((3, 64, 256), F32),
                pltpu.VMEM((3, 64, 256), F32),
                pltpu.VMEM((3, 2, 64, 256), BF16),
                pltpu.VMEM((2, 8, 128), F32),
                pltpu.VMEM((3, 2, 8, 128), F32),
                pltpu.VMEM((2, 2, 64, 128), F32),
                pltpu.VMEM((chunks, tokens, CW), BF16),
                pltpu.VMEM((2, 256, 128), BF16),
                pltpu.VMEM((chunks, 8, 64, CW), BF16),
                pltpu.VMEM((chunks, 7, 64, CW), BF16),
                pltpu.VMEM((chunks, 64, CW), BF16),
                pltpu.VMEM((chunks, 64, CW), BF16),
                pltpu.VMEM((chunks, 64, CW), F32),
                pltpu.VMEM((chunks, 8, CW), F32),
                pltpu.VMEM((chunks, 7, 8, CW), F32),
                dma((11,)),
                dma((3,)), dma((3,)), dma((3,)), dma((3,)), dma((3,)), dma((3,)), dma((2, 3)), dma((2, 3)),
                dma((chunks,)), dma((chunks,)),
                dma((chunks,)), dma((chunks,)), dma((chunks,)), dma((chunks,)),
                dma((chunks,)), dma((chunks,)),
            ],
            compiler_params=pltpu.CompilerParams(collective_id=0, has_side_effects=True),
            name="section_pair",
        )(
            enter_fwd.reshape(tokens, width),
            enter_rev.reshape(tokens, width),
            cot_rev.reshape(tokens, width),
            gain.reshape(2, width),
            proj_down.reshape(2, latent, width),
            proj_up.reshape(2, latent, width),
            master.reshape(2 * rows, width),
            moment.reshape(2 * rows, width),
            second.reshape(2 * rows, width),
        )
        leave, codes, scales = pl.pallas_call(
            functools.partial(store, chunks),
            out_shape=(
                jax.ShapeDtypeStruct((tokens, width), BF16),
                jax.ShapeDtypeStruct((2 * rows, width), BF16),
                jax.ShapeDtypeStruct((2, 2, width // 128), F32),
            ),
            in_specs=[vmem_spec] * 3,
            out_specs=(any_spec,) * 3,
            scratch_shapes=[dma((2 * chunks + 1,))],
            compiler_params=pltpu.CompilerParams(vmem_limit_bytes=1 << 20),
            name="store_outputs",
        )(leave, codes, scales)
        return (
            leave.reshape(1, tokens, width),
            codes.reshape(2, 1, rows, width),
            scales.reshape(2, 1, 2, width // 128),
        )

    in_specs = (
        P("pipe", "expert", "dp"),
        P("pipe", "expert", "dp"),
        P("pipe", "expert", "dp"),
        P(None, "pipe", "dp"),
        P(None, "pipe", None, "dp"),
        P(None, "pipe", None, "dp"),
        P(None, "pipe", "expert", "dp"),
        P(None, "pipe", "expert", "dp"),
        P(None, "pipe", "expert", "dp"),
    )
    out_specs = (
        P("pipe", "expert", "dp"),
        P(None, "pipe", "expert", "dp"),
        P(None, "pipe", None, "dp"),
    )
    return jax.shard_map(shards, mesh=mesh, in_specs=in_specs, out_specs=out_specs, check_vma=False)
```
